32 devices in a mesh: dp: 8 (over z, x), seq: 4 (over y, core).
Axes of the slice: x: 2, y: 2, z: 4, core: 2. Of those that a mesh axis runs over, the one named last changes fastest.
Arguments:
- tokens: float32 [16, 256, 1024], P('dp', 'seq'), may hold values from -6 to 6
- output_cotangent: float32 [16, 256, 1024], P('dp', 'seq'), may hold values from -0.5 to 0.5
- placement: int32 [8], replicated, may hold values from 0 to 15, as said below
- inward: float32 [1024, 3072], P(('dp', 'seq'))
- outward: float32 [1024, 1024], P(('dp', 'seq')), may hold values from -0.75 to 0.75
- attend_vectors: float32 [5, 1024], P(None, ('dp', 'seq'))
- expand: float32 [1024, 4096], P(('dp', 'seq')), may hold values from -0.1875 to 0.1875
- shrink: float32 [4096, 1024], P(('dp', 'seq')), may hold values from -0.09375 to 0.09375
- feed_vectors: float32 [3, 1024], P(None, ('dp', 'seq'))
- expand_bias: float32 [4096], P(('dp', 'seq')), may hold values from -3 to 3
- inward_moments: float32 [2, 1024, 3072], P(None, ('dp', 'seq')), as said below
- outward_moments: float32 [2, 1024, 1024], P(None, ('dp', 'seq'))
- attend_moments: float32 [2, 5, 1024], P(None, None, ('dp', 'seq'))
- expand_moments: float32 [2, 1024, 4096], P(None, ('dp', 'seq'))
- shrink_moments: float32 [2, 4096, 1024], P(None, ('dp', 'seq'))
- feed_moments: float32 [2, 3, 1024], P(None, None, ('dp', 'seq'))
- bias_moments: float32 [2, 4096], P(None, ('dp', 'seq'))
Outputs:
- block_output: float32 [16, 256, 1024], P('dp', 'seq')
- input_gradient: float32 [16, 256, 1024], P('dp', 'seq')
- inward_gradient: float32 [1024, 3072], P(('dp', 'seq'))
- outward_gradient: float32 [1024, 1024], P(('dp', 'seq'))
- attend_gradient: float32 [5, 1024], P(None, ('dp', 'seq'))
- expand_gradient: float32 [1024, 4096], P(('dp', 'seq'))
- shrink_gradient: float32 [4096, 1024], P(('dp', 'seq'))
- feed_gradient: float32 [3, 1024], P(None, ('dp', 'seq'))
- bias_gradient: float32 [4096], P(('dp', 'seq'))
- inward_new: float32 [1024, 3072], P(('dp', 'seq'))
- outward_new: float32 [1024, 1024], P(('dp', 'seq'))
- attend_new: float32 [5, 1024], P(None, ('dp', 'seq'))
- expand_new: float32 [1024, 4096], P(('dp', 'seq'))
- shrink_new: float32 [4096, 1024], P(('dp', 'seq'))
- feed_new: float32 [3, 1024], P(None, ('dp', 'seq'))
- bias_new: float32 [4096], P(('dp', 'seq'))
- inward_state: float32 [2, 1024, 3072], P(None, ('dp', 'seq'))
- outward_state: float32 [2, 1024, 1024], P(None, ('dp', 'seq'))
- attend_state: float32 [2, 5, 1024], P(None, None, ('dp', 'seq'))
- expand_state: float32 [2, 1024, 4096], P(None, ('dp', 'seq'))
- shrink_state: float32 [2, 4096, 1024], P(None, ('dp', 'seq'))
- feed_state: float32 [2, 3, 1024], P(None, None, ('dp', 'seq'))
- bias_state: float32 [2, 4096], P(None, ('dp', 'seq'))
The draws below stay inside these ranges and needn't reach their ends.
Inputs may be any that keep to these rules, and one draw needn't show every extreme that they name: `placement`: entries are distinct slot numbers; slot s belongs to index s // 2 of dp; in every draw some index of dp holds 2 sequences. `inward_moments`: the second moment (index 1) is positive.
All inputs are finite; a program needn't handle non-finite values.
Results may differ from the reference program's by a relative error of at most 0.012.
Values may be sent and summed in bfloat16 or wider, within the bound.
A program may use at most 192 MiB of HBM per device.

```python
import math
import jax
import jax.numpy as jnp
from jax import lax

D = 1024
HEADS = 16
HEAD_DIM = 64
FF = 4096
LEN = 256
SLOTS = 2
SLOTS_ALL = 16
NSEQ = 8


def moments_draw(key, shape):
    first_moment = 2.0 * jax.random.normal(jax.random.fold_in(key, 11), shape, jnp.float32)
    second = jnp.exp(jax.random.uniform(jax.random.fold_in(key, 12), shape, jnp.float32, -1.386, 1.386))
    return jnp.stack([first_moment, second])


def vectors_draw(key, count):
    gains = 1.0 + 0.2 * jax.random.normal(jax.random.fold_in(key, 21), (1, D), jnp.float32)
    others = 0.5 * jax.random.normal(jax.random.fold_in(key, 22), (count - 1, D), jnp.float32)
    return jnp.concatenate([gains, others], axis=0)


def draw_placement(key, part):
    shuffled = jax.random.permutation(jax.random.fold_in(key, 3), SLOTS_ALL)
    ranking = jnp.zeros((SLOTS_ALL,), jnp.int32).at[shuffled].set(jnp.arange(SLOTS_ALL, dtype=jnp.int32))
    chosen = jax.random.randint(jax.random.fold_in(key, 4), (), 0, SLOTS_ALL // SLOTS)
    slot_ids = jnp.arange(SLOTS_ALL, dtype=jnp.int32)
    priority = jnp.where(slot_ids // SLOTS == chosen, slot_ids % SLOTS - SLOTS, ranking)
    return jnp.argsort(priority)[:NSEQ].astype(jnp.int32)


def draw_inward(key, part):
    base = jax.random.normal(jax.random.fold_in(key, 1), (D, 3 * D), jnp.float32) * D ** (-0.5)
    return base


def draw_attend_vectors(key, part):
    return vectors_draw(key, 5)


def draw_feed_vectors(key, part):
    return vectors_draw(key, 3)


def draw_inward_moments(key, part):
    return moments_draw(key, (D, 3 * D))


def draw_outward_moments(key, part):
    return moments_draw(key, (D, D))


def draw_attend_moments(key, part):
    return moments_draw(key, (5, D))


def draw_expand_moments(key, part):
    return moments_draw(key, (D, FF))


def draw_shrink_moments(key, part):
    return moments_draw(key, (FF, D))


def draw_feed_moments(key, part):
    return moments_draw(key, (3, D))


def draw_bias_moments(key, part):
    return moments_draw(key, (FF,))


def shard_levels(own_key, dims, shards, low, largest):
    def one(dim, parts):
        steps = jax.random.uniform(jax.random.fold_in(jax.random.fold_in(own_key, 6), dim), (parts,), jnp.float32, low / len(shards), largest / len(shards))
        return jnp.repeat(jnp.exp(steps), dims[dim] // parts).reshape((-1,) + (1,) * (len(dims) - dim - 1))

    loudness = one(*shards[0])
    for cut in shards[1:]:
        loudness = loudness * one(*cut)
    return loudness


def scatter_about(stream_key, dims, deviation, limit, pieces=(), kind=jnp.bfloat16):
    array = jax.random.normal(stream_key, dims, jnp.float32) * deviation
    if len(pieces) > 0:
        array = shard_levels(stream_key, dims, pieces, -0.22, 0.18) * array
    return jnp.clip(array, min=-limit, max=limit).astype(kind)


def setup_inputs(seed: int = 0) -> dict:
    splits = jax.random.split(jax.random.key(seed), 18)
    tokens = scatter_about(splits[0], (SLOTS_ALL, LEN, D), 1.0, 6.0, ((0, 8), (1, 4)), jnp.float32)
    output_cotangent = scatter_about(splits[1], (SLOTS_ALL, LEN, D), (4.0 / (NSEQ * LEN) ** 0.5), 0.5, ((0, 8), (1, 4)), jnp.float32)
    placement = draw_placement(jax.random.fold_in(splits[17], 71), 0)
    inward = draw_inward(jax.random.fold_in(splits[17], 71), 0)
    outward = scatter_about(splits[4], (D, D), (D // 16) ** -0.5, 0.75, ((0, 32),), jnp.float32)
    attend_vectors = draw_attend_vectors(jax.random.fold_in(splits[17], 71), 0)
    expand = scatter_about(splits[6], (D, FF), D ** -0.5, 0.1875, ((0, 32),), jnp.float32)
    shrink = scatter_about(splits[7], (FF, D), FF ** -0.5, 0.09375, ((0, 32),), jnp.float32)
    feed_vectors = draw_feed_vectors(jax.random.fold_in(splits[17], 71), 0)
    expand_bias = scatter_about(splits[9], (FF,), 0.5, 3.0, ((0, 32),), jnp.float32)
    inward_moments = draw_inward_moments(jax.random.fold_in(splits[17], 71), 0)
    outward_moments = draw_outward_moments(jax.random.fold_in(splits[17], 71), 0)
    attend_moments = draw_attend_moments(jax.random.fold_in(splits[17], 71), 0)
    expand_moments = draw_expand_moments(jax.random.fold_in(splits[17], 71), 0)
    shrink_moments = draw_shrink_moments(jax.random.fold_in(splits[17], 71), 0)
    feed_moments = draw_feed_moments(jax.random.fold_in(splits[17], 71), 0)
    bias_moments = draw_bias_moments(jax.random.fold_in(splits[17], 71), 0)
    return {"tokens": tokens, "output_cotangent": output_cotangent, "placement": placement, "inward": inward, "outward": outward, "attend_vectors": attend_vectors, "expand": expand, "shrink": shrink, "feed_vectors": feed_vectors, "expand_bias": expand_bias, "inward_moments": inward_moments, "outward_moments": outward_moments, "attend_moments": attend_moments, "expand_moments": expand_moments, "shrink_moments": shrink_moments, "feed_moments": feed_moments, "bias_moments": bias_moments}


norm_epsilon = 1e-05
beta_first = 0.9
beta_second = 0.95
adam_epsilon = 1e-08
learn_rate = 0.01
weight_decay = 0.1
adam_steps = 4
gelu_scale = 0.7978845608028654
gelu_cubic = 0.044715
masked_score = -1e+30

def halved(operand):
    return operand.astype(jnp.bfloat16)

def normalize(operand):
    average = lax.optimization_barrier(jnp.mean(operand, axis=-1, keepdims=True))
    centered = operand - average
    variance = lax.optimization_barrier(jnp.mean(centered * centered, axis=-1, keepdims=True))
    inverse = lax.rsqrt(variance + norm_epsilon)
    return (centered * inverse, inverse)

def norm_back(upstream, normed, inverse):
    first_mean = lax.optimization_barrier(jnp.mean(upstream, axis=-1, keepdims=True))
    second_mean = lax.optimization_barrier(jnp.mean(upstream * normed, axis=-1, keepdims=True))
    return inverse * (upstream - first_mean - normed * second_mean)

def gelu_pair(upper):
    inner_arg = gelu_scale * (upper + gelu_cubic * upper * upper * upper)
    tangent = jnp.tanh(inner_arg)
    active = 0.5 * upper * (1.0 + tangent)
    slope = 0.5 * (1.0 + tangent) + 0.5 * upper * (1.0 - tangent * tangent) * gelu_scale * (1.0 + 3.0 * gelu_cubic * upper * upper)
    return (active, slope)

def adamw_update(parameter, gradient, moments, decay_rate):
    first_moment = beta_first * moments[0] + (1.0 - beta_first) * gradient
    second = beta_second * moments[1] + (1.0 - beta_second) * gradient * gradient
    unbiased_first = first_moment / (1.0 - beta_first ** adam_steps)
    unbiased_second = second / (1.0 - beta_second ** adam_steps)
    update = unbiased_first / (jnp.sqrt(unbiased_second) + adam_epsilon) + decay_rate * parameter
    return (parameter - learn_rate * update, jnp.stack([first_moment, second]))

def forward_backward(weights, tokens, cotangent):
    proj_in, proj_out, vectors_one, proj_up, proj_down, vectors_two, bias_up = weights
    highest = lax.Precision.HIGHEST
    length = tokens.shape[0]
    model_width = tokens.shape[1]
    score_scale = 1.0 / math.sqrt(HEAD_DIM)
    vec_one = vectors_one.astype(jnp.float32)
    vec_two = vectors_two.astype(jnp.float32)
    normed_one, inverse_one = normalize(tokens)
    lifted_one = halved(normed_one * vec_one[0] + vec_one[1])
    packed = jnp.dot(lifted_one, proj_in, preferred_element_type=jnp.float32)
    queries = halved(packed[:, :model_width] + vec_one[2])
    key_half = halved(packed[:, model_width:2 * model_width])
    value_half = halved(packed[:, 2 * model_width:] + vec_one[3])
    query_heads = queries.astype(jnp.float32).reshape(length, HEADS, HEAD_DIM)
    key_heads = key_half.astype(jnp.float32).reshape(length, HEADS, HEAD_DIM)
    value_heads = value_half.astype(jnp.float32).reshape(length, HEADS, HEAD_DIM)
    positions = jnp.arange(length)
    allowed = positions[None, :] <= positions[:, None]
    scores = jnp.einsum('qhd,khd->hqk', query_heads, key_heads, precision=highest) * score_scale
    scores = jnp.where(allowed[None], scores, masked_score)
    score_peak = lax.optimization_barrier(jnp.max(scores, axis=-1, keepdims=True))
    log_total = score_peak + jnp.log(lax.optimization_barrier(jnp.sum(jnp.exp(scores - score_peak), axis=-1, keepdims=True)))
    weights_full = jnp.exp(scores - log_total)
    weights_half = halved(weights_full)
    attended = halved(jnp.einsum('hqk,khd->qhd', weights_half.astype(jnp.float32), value_heads, precision=highest).reshape(length, model_width))
    middle = tokens + jnp.dot(attended, proj_out, preferred_element_type=jnp.float32) + vec_one[4]
    normed_two, inverse_two = normalize(middle)
    lifted_two = halved(normed_two * vec_two[0] + vec_two[1])
    upper_act = jnp.dot(lifted_two, proj_up, preferred_element_type=jnp.float32) + bias_up.astype(jnp.float32)
    active_full, gelu_slope = gelu_pair(upper_act)
    active = halved(active_full)
    block_out = middle + jnp.dot(active, proj_down, preferred_element_type=jnp.float32) + vec_two[2]
    cot_half = halved(cotangent)
    shrink_grad = jnp.dot(active.T, cot_half, preferred_element_type=jnp.float32)
    feed_bias_grad = lax.optimization_barrier(jnp.sum(cotangent, axis=0))
    upper_grad = jnp.dot(cot_half, proj_down.T, preferred_element_type=jnp.float32) * gelu_slope
    upper_half = halved(upper_grad)
    expand_grad = jnp.dot(lifted_two.T, upper_half, preferred_element_type=jnp.float32)
    expand_bias_grad = lax.optimization_barrier(jnp.sum(upper_grad, axis=0))
    lift_two_grad = jnp.dot(upper_half, proj_up.T, preferred_element_type=jnp.float32)
    gain_two_grad = lax.optimization_barrier(jnp.sum(lift_two_grad * normed_two, axis=0))
    shift_two_grad = lax.optimization_barrier(jnp.sum(lift_two_grad, axis=0))
    middle_grad = cotangent + norm_back(lift_two_grad * vec_two[0], normed_two, inverse_two)
    middle_half = halved(middle_grad)
    outward_grad = jnp.dot(attended.T, middle_half, preferred_element_type=jnp.float32)
    out_bias_grad = lax.optimization_barrier(jnp.sum(middle_grad, axis=0))
    attended_grad = halved(jnp.dot(middle_half, proj_out.T, preferred_element_type=jnp.float32))
    grad_heads = attended_grad.astype(jnp.float32).reshape(length, HEADS, HEAD_DIM)
    attended_heads = attended.astype(jnp.float32).reshape(length, HEADS, HEAD_DIM)
    delta_sum = lax.optimization_barrier(jnp.sum(grad_heads * attended_heads, axis=-1))
    weight_grad = jnp.einsum('qhd,khd->hqk', grad_heads, value_heads, precision=highest)
    score_grad = halved(weights_full * (weight_grad - delta_sum.T[:, :, None]) * score_scale).astype(jnp.float32)
    query_grad = jnp.einsum('hqk,khd->qhd', score_grad, key_heads, precision=highest).reshape(length, model_width)
    key_grad = jnp.einsum('hqk,qhd->khd', score_grad, query_heads, precision=highest).reshape(length, model_width)
    value_grad = jnp.einsum('hqk,qhd->khd', weights_half.astype(jnp.float32), grad_heads, precision=highest).reshape(length, model_width)
    packed_grad = halved(jnp.concatenate([query_grad, key_grad, value_grad], axis=1))
    inward_grad = jnp.dot(lifted_one.T, packed_grad, preferred_element_type=jnp.float32)
    query_bias_grad = lax.optimization_barrier(jnp.sum(query_grad, axis=0))
    value_bias_grad = lax.optimization_barrier(jnp.sum(value_grad, axis=0))
    lift_one_grad = jnp.dot(packed_grad, proj_in.T, preferred_element_type=jnp.float32)
    gain_one_grad = lax.optimization_barrier(jnp.sum(lift_one_grad * normed_one, axis=0))
    shift_one_grad = lax.optimization_barrier(jnp.sum(lift_one_grad, axis=0))
    tokens_grad = middle_grad + norm_back(lift_one_grad * vec_one[0], normed_one, inverse_one)
    gradients = (inward_grad, outward_grad, jnp.stack([gain_one_grad, shift_one_grad, query_bias_grad, value_bias_grad, out_bias_grad]), expand_grad, shrink_grad, jnp.stack([gain_two_grad, shift_two_grad, feed_bias_grad]), expand_bias_grad)
    return (block_out, tokens_grad, gradients)

def reference(tokens, output_cotangent, placement, inward, outward, attend_vectors, expand, shrink, feed_vectors, expand_bias, inward_moments, outward_moments, attend_moments, expand_moments, shrink_moments, feed_moments, bias_moments):
    masters = (inward, outward, attend_vectors, expand, shrink, feed_vectors, expand_bias)
    rounded = tuple((halved(member) for member in masters))
    live_tokens = tokens[placement]
    live_cot = output_cotangent[placement]
    zero_grads = tuple((jnp.zeros(member.shape, jnp.float32) for member in masters))

    def visit(totals, inputs_pair):
        block_out, tokens_grad, gradients = forward_backward(rounded, inputs_pair[0], inputs_pair[1])
        summed = tuple((left + right for left, right in zip(totals, gradients)))
        return (summed, (block_out, tokens_grad))
    totals, (outputs, input_grads) = lax.scan(visit, zero_grads, (live_tokens, live_cot))
    block_output = jnp.zeros(tokens.shape, jnp.float32).at[placement].set(outputs)
    input_gradient = jnp.zeros(tokens.shape, jnp.float32).at[placement].set(input_grads)
    moments_all = (inward_moments, outward_moments, attend_moments, expand_moments, shrink_moments, feed_moments, bias_moments)
    decays = (weight_decay, weight_decay, 0.0, weight_decay, weight_decay, 0.0, 0.0)
    fresh = []
    states = []
    for index_item in range(7):
        new_param, new_state = adamw_update(masters[index_item], totals[index_item], moments_all[index_item], decays[index_item])
        fresh.append(new_param)
        states.append(new_state)
    return (block_output, input_gradient, totals[0], totals[1], totals[2], totals[3], totals[4], totals[5], totals[6], fresh[0], fresh[1], fresh[2], fresh[3], fresh[4], fresh[5], fresh[6], states[0], states[1], states[2], states[3], states[4], states[5], states[6])
```

```python
import math

import jax
import jax.numpy as jnp
from jax import lax
from jax.sharding import PartitionSpec as P

HEADS = 16
HEAD_DIM = 64


norm_epsilon = 1e-05
beta_first = 0.9
beta_second = 0.95
adam_epsilon = 1e-08
learn_rate = 0.01
weight_decay = 0.1
adam_steps = 4
gelu_scale = 0.7978845608028654
gelu_cubic = 0.044715
masked_score = -1e30


def halved(operand):
    return operand.astype(jnp.bfloat16)


def normalize(operand):
    average = jnp.mean(operand, axis=-1, keepdims=True)
    centered = operand - average
    variance = jnp.mean(centered * centered, axis=-1, keepdims=True)
    inverse = lax.rsqrt(variance + norm_epsilon)
    return (centered * inverse, inverse)


def norm_back(upstream, normed, inverse):
    first_mean = jnp.mean(upstream, axis=-1, keepdims=True)
    second_mean = jnp.mean(upstream * normed, axis=-1, keepdims=True)
    return inverse * (upstream - first_mean - normed * second_mean)


def gelu_pair(upper):
    inner_arg = gelu_scale * (upper + gelu_cubic * upper * upper * upper)
    tangent = jnp.tanh(inner_arg)
    active = 0.5 * upper * (1.0 + tangent)
    slope = 0.5 * (1.0 + tangent) + 0.5 * upper * (1.0 - tangent * tangent) * gelu_scale * (
        1.0 + 3.0 * gelu_cubic * upper * upper
    )
    return (active, slope)


def adamw_update(parameter, gradient, moments, decay_rate):
    first_moment = beta_first * moments[0] + (1.0 - beta_first) * gradient
    second = beta_second * moments[1] + (1.0 - beta_second) * gradient * gradient
    unbiased_first = first_moment / (1.0 - beta_first**adam_steps)
    unbiased_second = second / (1.0 - beta_second**adam_steps)
    update = unbiased_first / (jnp.sqrt(unbiased_second) + adam_epsilon) + decay_rate * parameter
    return (parameter - learn_rate * update, jnp.stack([first_moment, second]))


def spread_columns(piece, groups, inner):
    rows = piece.shape[0]
    parts = piece.reshape(rows, -1, groups, inner)
    moved = lax.all_to_all(parts, "seq", 2, 0, tiled=True)
    return moved.reshape(groups * rows, -1)


def collect_columns(piece, groups, inner):
    rows = piece.shape[0] // groups
    parts = piece.reshape(rows * groups, -1, 1, inner)
    moved = lax.all_to_all(parts, "seq", 0, 2, tiled=True)
    return moved.reshape(rows, -1)


def body(
    tokens,
    output_cotangent,
    placement,
    inward,
    outward,
    attend_vectors,
    expand,
    shrink,
    feed_vectors,
    expand_bias,
    inward_moments,
    outward_moments,
    attend_moments,
    expand_moments,
    shrink_moments,
    feed_moments,
    bias_moments,
):
    slot_count, block_size, model_width = tokens.shape
    groups = lax.axis_size("seq")
    replicas = lax.axis_size("dp")
    devices = groups * replicas
    mine = lax.axis_index("seq")
    length = block_size * groups
    row_count = slot_count * block_size
    all_rows = slot_count * length
    head_count = HEADS // groups
    part_width = head_count * HEAD_DIM
    vec_width = attend_vectors.shape[1]
    hidden_part = expand_bias.shape[0]
    score_scale = 1.0 / math.sqrt(HEAD_DIM)
    whole = ("dp", "seq")

    def gather_rows(local):
        full = lax.all_gather(
            local.reshape(slot_count, block_size, -1), "seq", axis=1, tiled=True
        )
        return full.reshape(all_rows, -1)

    def scatter_rows(partial):
        own = lax.psum_scatter(
            halved(partial).reshape(slot_count, length, -1), "seq", scatter_dimension=1, tiled=True
        )
        return own.reshape(row_count, -1).astype(jnp.float32)

    slot_ids = lax.axis_index("dp") * slot_count + jnp.arange(slot_count, dtype=jnp.int32)
    live_mask = jnp.any(placement[None, :] == slot_ids[:, None], axis=1).astype(jnp.float32)[
        :, None, None
    ]

    small = jnp.concatenate(
        [
            halved(attend_vectors).reshape(-1),
            halved(feed_vectors).reshape(-1),
            halved(expand_bias),
        ]
    )
    small_rows = 16
    small_block = jnp.pad(small, (0, small_rows * model_width - small.shape[0])).reshape(
        small_rows, model_width
    )
    out_rows = outward.shape[0]
    first = lax.all_gather(
        jnp.concatenate([halved(outward), small_block], axis=0), whole, axis=0, tiled=True
    ).reshape(devices, out_rows + small_rows, model_width)
    out_whole = first[:, :out_rows].reshape(devices * out_rows, model_width)
    small_all = first[:, out_rows:].reshape(devices, -1)[:, : small.shape[0]].astype(jnp.float32)
    vectors = jnp.transpose(
        small_all[:, : 8 * vec_width].reshape(devices, 8, vec_width), (1, 0, 2)
    ).reshape(8, model_width)
    vec_one = vectors[:5]
    vec_two = vectors[5:]
    bias_all = small_all[:, 8 * vec_width :].reshape(replicas, groups, hidden_part)
    bias_part = lax.dynamic_index_in_dim(bias_all, mine, 1, keepdims=False).reshape(-1)

    in_width = 3 * part_width
    moved_in = spread_columns(halved(inward), groups, part_width)
    moved_up = spread_columns(halved(expand), groups, hidden_part)
    in_part = lax.all_gather(moved_in, "dp", axis=0, tiled=True)
    up_part = lax.all_gather(moved_up, "dp", axis=0, tiled=True)
    down_part = lax.all_gather(halved(shrink), "dp", axis=0, tiled=True)

    cotangent = (output_cotangent * live_mask).reshape(row_count, model_width)
    cot_all = gather_rows(halved(cotangent))
    feed_bias_grad = jnp.sum(cotangent, axis=0)

    flat_tokens = tokens.reshape(row_count, model_width)
    normed_one, inverse_one = normalize(flat_tokens)
    lifted_one = gather_rows(halved(normed_one * vec_one[0] + vec_one[1]))
    packed = jnp.dot(lifted_one, in_part, preferred_element_type=jnp.float32)
    bias_query = lax.dynamic_slice_in_dim(vec_one[2], mine * part_width, part_width)
    bias_value = lax.dynamic_slice_in_dim(vec_one[3], mine * part_width, part_width)

    def to_heads(operand):
        return jnp.transpose(
            operand.reshape(slot_count, length, head_count, HEAD_DIM), (0, 2, 1, 3)
        )

    def from_heads(operand):
        return jnp.transpose(operand, (0, 2, 1, 3)).reshape(all_rows, part_width)

    queries = to_heads(halved(packed[:, :part_width] + bias_query))
    keys = to_heads(halved(packed[:, part_width : 2 * part_width]))
    values = to_heads(halved(packed[:, 2 * part_width :] + bias_value))
    positions = jnp.arange(length)
    allowed = positions[None, :] <= positions[:, None]
    scores = (
        jnp.einsum("shqd,shkd->shqk", queries, keys, preferred_element_type=jnp.float32)
        * score_scale
    )
    scores = jnp.where(allowed, scores, masked_score)
    score_peak = jnp.max(scores, axis=-1, keepdims=True)
    log_total = score_peak + jnp.log(jnp.sum(jnp.exp(scores - score_peak), axis=-1, keepdims=True))
    weights_full = jnp.exp(scores - log_total)
    weights_half = halved(weights_full)
    attended_heads = halved(
        jnp.einsum("shqk,shkd->shqd", weights_half, values, preferred_element_type=jnp.float32)
    )
    attended = lax.all_to_all(
        from_heads(attended_heads).reshape(slot_count, length, part_width), "seq", 1, 2, tiled=True
    ).reshape(row_count, model_width)
    projected = jnp.dot(attended, out_whole, preferred_element_type=jnp.float32)
    middle = flat_tokens + projected + vec_one[4]
    normed_two, inverse_two = normalize(middle)
    lifted_two = gather_rows(halved(normed_two * vec_two[0] + vec_two[1]))
    upper = jnp.dot(lifted_two, up_part, preferred_element_type=jnp.float32) + bias_part
    active_full, slope = gelu_pair(upper)
    active = halved(active_full)
    upper_grad = (
        lax.dot_general(
            cot_all, down_part, (((1,), (1,)), ((), ())), preferred_element_type=jnp.float32
        )
        * slope
    )
    upper_half = halved(upper_grad)
    lift_two_grad = scatter_rows(
        lax.dot_general(
            upper_half, up_part, (((1,), (1,)), ((), ())), preferred_element_type=jnp.float32
        )
    )
    fed = scatter_rows(jnp.dot(active, down_part, preferred_element_type=jnp.float32))
    block_output = (middle + fed + vec_two[2]).reshape(
        slot_count, block_size, model_width
    ) * live_mask

    def outer(left, right):
        return halved(
            lax.dot_general(
                left, right, (((0,), (0,)), ((), ())), preferred_element_type=jnp.float32
            )
        )

    shrink_sum = lax.psum_scatter(
        outer(active, cot_all), "dp", scatter_dimension=0, tiled=True
    ).astype(jnp.float32)
    expand_sum = collect_columns(
        lax.psum_scatter(outer(lifted_two, upper_half), "dp", scatter_dimension=0, tiled=True),
        groups,
        hidden_part,
    ).astype(jnp.float32)
    bias_grad = jnp.sum(upper_grad, axis=0).reshape(replicas, 1, hidden_part)

    gain_two_grad = jnp.sum(lift_two_grad * normed_two, axis=0)
    shift_two_grad = jnp.sum(lift_two_grad, axis=0)
    middle_grad = cotangent + norm_back(lift_two_grad * vec_two[0], normed_two, inverse_two)
    middle_half = halved(middle_grad)
    out_bias_grad = jnp.sum(middle_grad, axis=0)
    attended_back = halved(
        lax.dot_general(
            middle_half, out_whole, (((1,), (1,)), ((), ())), preferred_element_type=jnp.float32
        )
    )
    attended_grad = to_heads(
        lax.all_to_all(
            attended_back.reshape(slot_count, block_size, model_width), "seq", 2, 1, tiled=True
        ).reshape(all_rows, part_width)
    )
    outward_sum = lax.psum_scatter(
        outer(attended, middle_half), whole, scatter_dimension=0, tiled=True
    ).astype(jnp.float32)
    delta_sum = jnp.sum(
        attended_grad.astype(jnp.float32) * attended_heads.astype(jnp.float32),
        axis=-1,
        keepdims=True,
    )
    weight_grad = jnp.einsum(
        "shqd,shkd->shqk", attended_grad, values, preferred_element_type=jnp.float32
    )
    score_grad = halved(weights_full * (weight_grad - delta_sum) * score_scale)
    query_grad = from_heads(
        jnp.einsum("shqk,shkd->shqd", score_grad, keys, preferred_element_type=jnp.float32)
    )
    key_grad = from_heads(
        jnp.einsum("shqk,shqd->shkd", score_grad, queries, preferred_element_type=jnp.float32)
    )
    value_grad = from_heads(
        jnp.einsum(
            "shqk,shqd->shkd", weights_half, attended_grad, preferred_element_type=jnp.float32
        )
    )
    packed_grad = halved(jnp.concatenate([query_grad, key_grad, value_grad], axis=1))
    lift_one_grad = scatter_rows(
        lax.dot_general(
            packed_grad, in_part, (((1,), (1,)), ((), ())), preferred_element_type=jnp.float32
        )
    )
    inward_sum = collect_columns(
        lax.psum_scatter(outer(lifted_one, packed_grad), "dp", scatter_dimension=0, tiled=True),
        groups,
        part_width,
    ).astype(jnp.float32)

    def place_part(part):
        return lax.dynamic_update_slice_in_dim(
            jnp.zeros((model_width,), jnp.float32), part, mine * part_width, 0
        )

    gain_one_grad = jnp.sum(lift_one_grad * normed_one, axis=0)
    shift_one_grad = jnp.sum(lift_one_grad, axis=0)
    tokens_grad = middle_grad + norm_back(lift_one_grad * vec_one[0], normed_one, inverse_one)
    input_gradient = tokens_grad.reshape(slot_count, block_size, model_width) * live_mask
    vector_grads = jnp.stack(
        [
            gain_one_grad,
            shift_one_grad,
            place_part(jnp.sum(query_grad, axis=0)),
            place_part(jnp.sum(value_grad, axis=0)),
            out_bias_grad,
            gain_two_grad,
            shift_two_grad,
            feed_bias_grad,
        ]
    ).T
    bias_placed = lax.dynamic_update_slice_in_dim(
        jnp.zeros((replicas, groups, hidden_part), jnp.float32), bias_grad, mine, 1
    ).reshape(model_width, -1)
    small_sum = lax.psum_scatter(
        jnp.concatenate([vector_grads, bias_placed], axis=1),
        whole,
        scatter_dimension=0,
        tiled=True,
    )
    attend_vec_sum = small_sum[:, :5].T
    feed_vec_sum = small_sum[:, 5:8].T
    bias_sum = small_sum[:, 8:].reshape(-1)
    inward_new, inward_state = adamw_update(inward, inward_sum, inward_moments, weight_decay)
    outward_new, outward_state = adamw_update(outward, outward_sum, outward_moments, weight_decay)
    attend_new, attend_state = adamw_update(attend_vectors, attend_vec_sum, attend_moments, 0.0)
    expand_new, expand_state = adamw_update(expand, expand_sum, expand_moments, weight_decay)
    shrink_new, shrink_state = adamw_update(shrink, shrink_sum, shrink_moments, weight_decay)
    feed_new, feed_state = adamw_update(feed_vectors, feed_vec_sum, feed_moments, 0.0)
    bias_new, bias_state = adamw_update(expand_bias, bias_sum, bias_moments, 0.0)
    return (
        block_output,
        input_gradient,
        inward_sum,
        outward_sum,
        attend_vec_sum,
        expand_sum,
        shrink_sum,
        feed_vec_sum,
        bias_sum,
        inward_new,
        outward_new,
        attend_new,
        expand_new,
        shrink_new,
        feed_new,
        bias_new,
        inward_state,
        outward_state,
        attend_state,
        expand_state,
        shrink_state,
        feed_state,
        bias_state,
    )


def solution(mesh):
    placed = (
        P("dp", "seq", None),
        P("dp", "seq", None),
        P(),
        P(("dp", "seq"), None),
        P(("dp", "seq"), None),
        P(None, ("dp", "seq")),
        P(("dp", "seq"), None),
        P(("dp", "seq"), None),
        P(None, ("dp", "seq")),
        P(("dp", "seq")),
        P(None, ("dp", "seq"), None),
        P(None, ("dp", "seq"), None),
        P(None, None, ("dp", "seq")),
        P(None, ("dp", "seq"), None),
        P(None, ("dp", "seq"), None),
        P(None, None, ("dp", "seq")),
        P(None, ("dp", "seq")),
    )
    return jax.shard_map(
        body,
        mesh=mesh,
        in_specs=placed,
        out_specs=(
            P("dp", "seq", None),
            P("dp", "seq", None),
            P(("dp", "seq"), None),
            P(("dp", "seq"), None),
            P(None, ("dp", "seq")),
            P(("dp", "seq"), None),
            P(("dp", "seq"), None),
            P(None, ("dp", "seq")),
            P(("dp", "seq")),
            P(("dp", "seq"), None),
            P(("dp", "seq"), None),
            P(None, ("dp", "seq")),
            P(("dp", "seq"), None),
            P(("dp", "seq"), None),
            P(None, ("dp", "seq")),
            P(("dp", "seq")),
            P(None, ("dp", "seq"), None),
            P(None, ("dp", "seq"), None),
            P(None, None, ("dp", "seq")),
            P(None, ("dp", "seq"), None),
            P(None, ("dp", "seq"), None),
            P(None, None, ("dp", "seq")),
            P(None, ("dp", "seq")),
        ),
        check_vma=False,
    )
```

```python
import math

import jax
import jax.numpy as jnp
from jax import lax
from jax.sharding import PartitionSpec as P

HEADS = 16
HEAD_DIM = 64


norm_epsilon = 1e-05
beta_first = 0.9
beta_second = 0.95
adam_epsilon = 1e-08
learn_rate = 0.01
weight_decay = 0.1
adam_steps = 4
gelu_scale = 0.7978845608028654
gelu_cubic = 0.044715
masked_score = -1e30


def halved(operand):
    return operand.astype(jnp.bfloat16)


def normalize(operand):
    average = jnp.mean(operand, axis=-1, keepdims=True)
    centered = operand - average
    variance = jnp.mean(centered * centered, axis=-1, keepdims=True)
    inverse = lax.rsqrt(variance + norm_epsilon)
    return (centered * inverse, inverse)


def norm_back(upstream, normed, inverse):
    first_mean = jnp.mean(upstream, axis=-1, keepdims=True)
    second_mean = jnp.mean(upstream * normed, axis=-1, keepdims=True)
    return inverse * (upstream - first_mean - normed * second_mean)


def gelu_pair(upper):
    inner_arg = gelu_scale * (upper + gelu_cubic * upper * upper * upper)
    tangent = jnp.tanh(inner_arg)
    active = 0.5 * upper * (1.0 + tangent)
    slope = 0.5 * (1.0 + tangent) + 0.5 * upper * (1.0 - tangent * tangent) * gelu_scale * (
        1.0 + 3.0 * gelu_cubic * upper * upper
    )
    return (active, slope)


def adamw_update(parameter, gradient, moments, decay_rate):
    first_moment = beta_first * moments[0] + (1.0 - beta_first) * gradient
    second = beta_second * moments[1] + (1.0 - beta_second) * gradient * gradient
    unbiased_first = first_moment / (1.0 - beta_first**adam_steps)
    unbiased_second = second / (1.0 - beta_second**adam_steps)
    update = unbiased_first / (jnp.sqrt(unbiased_second) + adam_epsilon) + decay_rate * parameter
    return (parameter - learn_rate * update, jnp.stack([first_moment, second]))


def collect_columns(piece, groups, inner):
    rows = piece.shape[0] // groups
    parts = piece.reshape(rows * groups, -1, 1, inner)
    moved = lax.all_to_all(parts, "seq", 0, 2, tiled=True)
    return moved.reshape(rows, -1)


def body(
    tokens,
    output_cotangent,
    placement,
    inward,
    outward,
    attend_vectors,
    expand,
    shrink,
    feed_vectors,
    expand_bias,
    inward_moments,
    outward_moments,
    attend_moments,
    expand_moments,
    shrink_moments,
    feed_moments,
    bias_moments,
):
    slot_count, block_size, model_width = tokens.shape
    groups = lax.axis_size("seq")
    replicas = lax.axis_size("dp")
    devices = groups * replicas
    mine = lax.axis_index("seq")
    length = block_size * groups
    row_count = slot_count * block_size
    all_rows = slot_count * length
    head_count = HEADS // groups
    part_width = head_count * HEAD_DIM
    vec_width = attend_vectors.shape[1]
    hidden_part = expand_bias.shape[0]
    score_scale = 1.0 / math.sqrt(HEAD_DIM)

    def gather_rows(local):
        full = lax.all_gather(
            local.reshape(slot_count, block_size, -1), "seq", axis=1, tiled=True
        )
        return full.reshape(all_rows, -1)

    def scatter_rows(partial):
        own = lax.psum_scatter(
            halved(partial).reshape(slot_count, length, -1), "seq", scatter_dimension=1, tiled=True
        )
        return own.reshape(row_count, -1).astype(jnp.float32)

    slot_ids = lax.axis_index("dp") * slot_count + jnp.arange(slot_count, dtype=jnp.int32)
    live_mask = jnp.any(placement[None, :] == slot_ids[:, None], axis=1).astype(jnp.float32)[
        :, None, None
    ]

    small = jnp.concatenate(
        [
            halved(attend_vectors).reshape(-1),
            halved(feed_vectors).reshape(-1),
            halved(expand_bias),
        ]
    )
    small_size = small.shape[0]
    pad_rows = 16
    in_rows = inward.shape[0]
    block_rows = groups * in_rows
    small_row = jnp.broadcast_to(
        jnp.pad(small, (0, model_width - small_size)), (groups, 1, model_width)
    )
    both = jnp.concatenate([halved(inward), halved(outward)], axis=1)
    both_parts = jnp.transpose(both.reshape(in_rows, -1, groups, part_width), (2, 0, 1, 3))
    up_parts = jnp.transpose(
        halved(expand).reshape(in_rows, replicas, groups, hidden_part), (2, 0, 1, 3)
    )
    moved = lax.all_to_all(
        jnp.concatenate(
            [
                both_parts.reshape(groups, in_rows, model_width),
                up_parts.reshape(groups, in_rows, model_width),
                small_row,
            ],
            axis=1,
        ),
        "seq",
        0,
        0,
        tiled=True,
    )
    small_block = jnp.pad(moved[:, 2 * in_rows], ((0, pad_rows - groups), (0, 0)))
    first = lax.all_gather(
        jnp.concatenate(
            [moved[:, :in_rows].reshape(block_rows, model_width), small_block], axis=0
        ),
        "dp",
        axis=0,
        tiled=True,
    ).reshape(replicas, block_rows + pad_rows, model_width)
    both_part = first[:, :block_rows].reshape(model_width, model_width)
    in_part = both_part[:, : 3 * part_width]
    out_part = both_part[:, 3 * part_width :]
    small_all = (
        first[:, block_rows : block_rows + groups, :small_size]
        .reshape(devices, small_size)
        .astype(jnp.float32)
    )
    vectors = jnp.transpose(
        small_all[:, : 8 * vec_width].reshape(devices, 8, vec_width), (1, 0, 2)
    ).reshape(8, model_width)
    vec_one = vectors[:5]
    vec_two = vectors[5:]
    bias_all = small_all[:, 8 * vec_width :].reshape(replicas, groups, hidden_part)
    bias_part = lax.dynamic_index_in_dim(bias_all, mine, 1, keepdims=False).reshape(-1)
    up_part = lax.all_gather(
        moved[:, in_rows : 2 * in_rows].reshape(block_rows, model_width),
        "dp",
        axis=0,
        tiled=True,
    )
    down_part = lax.all_gather(halved(shrink), "dp", axis=0, tiled=True)

    cotangent = (output_cotangent * live_mask).reshape(row_count, model_width)
    cot_all = gather_rows(halved(cotangent))
    feed_bias_grad = jnp.sum(cotangent, axis=0)

    flat_tokens = tokens.reshape(row_count, model_width)
    normed_one, inverse_one = normalize(flat_tokens)
    lifted_one = gather_rows(halved(normed_one * vec_one[0] + vec_one[1]))
    packed = jnp.dot(lifted_one, in_part, preferred_element_type=jnp.float32)
    bias_query = lax.dynamic_slice_in_dim(vec_one[2], mine * part_width, part_width)
    bias_value = lax.dynamic_slice_in_dim(vec_one[3], mine * part_width, part_width)

    def to_heads(operand):
        return jnp.transpose(
            operand.reshape(slot_count, length, head_count, HEAD_DIM), (0, 2, 1, 3)
        )

    def from_heads(operand):
        return jnp.transpose(operand, (0, 2, 1, 3)).reshape(all_rows, part_width)

    queries = to_heads(halved(packed[:, :part_width] + bias_query))
    keys = to_heads(halved(packed[:, part_width : 2 * part_width]))
    values = to_heads(halved(packed[:, 2 * part_width :] + bias_value))
    positions = jnp.arange(length)
    allowed = positions[None, :] <= positions[:, None]
    scores = (
        jnp.einsum("shqd,shkd->shqk", queries, keys, preferred_element_type=jnp.float32)
        * score_scale
    )
    scores = jnp.where(allowed, scores, masked_score)
    score_peak = jnp.max(scores, axis=-1, keepdims=True)
    log_total = score_peak + jnp.log(jnp.sum(jnp.exp(scores - score_peak), axis=-1, keepdims=True))
    weights_full = jnp.exp(scores - log_total)
    weights_half = halved(weights_full)
    attended_heads = halved(
        jnp.einsum("shqk,shkd->shqd", weights_half, values, preferred_element_type=jnp.float32)
    )
    attended = lax.all_gather(from_heads(attended_heads), "seq", axis=0, tiled=False)
    attended = jnp.transpose(attended, (1, 0, 2)).reshape(all_rows, model_width)
    projected = lax.all_to_all(
        halved(jnp.dot(attended, out_part, preferred_element_type=jnp.float32)).reshape(
            slot_count, length, part_width
        ),
        "seq",
        1,
        2,
        tiled=True,
    ).reshape(row_count, model_width)
    middle = flat_tokens + projected + vec_one[4]
    normed_two, inverse_two = normalize(middle)
    lifted_two = gather_rows(halved(normed_two * vec_two[0] + vec_two[1]))
    upper = jnp.dot(lifted_two, up_part, preferred_element_type=jnp.float32) + bias_part
    active_full, slope = gelu_pair(upper)
    active = halved(active_full)
    upper_grad = (
        lax.dot_general(
            cot_all, down_part, (((1,), (1,)), ((), ())), preferred_element_type=jnp.float32
        )
        * slope
    )
    upper_half = halved(upper_grad)
    lift_two_grad = scatter_rows(
        lax.dot_general(
            upper_half, up_part, (((1,), (1,)), ((), ())), preferred_element_type=jnp.float32
        )
    )
    fed = scatter_rows(jnp.dot(active, down_part, preferred_element_type=jnp.float32))
    block_output = (middle + fed + vec_two[2]).reshape(
        slot_count, block_size, model_width
    ) * live_mask

    def outer(left, right):
        return halved(
            lax.dot_general(
                left, right, (((0,), (0,)), ((), ())), preferred_element_type=jnp.float32
            )
        )

    shrink_sum = lax.psum_scatter(
        outer(active, cot_all), "dp", scatter_dimension=0, tiled=True
    ).astype(jnp.float32)
    expand_sum = collect_columns(
        lax.psum_scatter(outer(lifted_two, upper_half), "dp", scatter_dimension=0, tiled=True),
        groups,
        hidden_part,
    ).astype(jnp.float32)
    bias_grad = jnp.sum(upper_grad, axis=0).reshape(replicas, 1, hidden_part)

    gain_two_grad = jnp.sum(lift_two_grad * normed_two, axis=0)
    shift_two_grad = jnp.sum(lift_two_grad, axis=0)
    middle_grad = cotangent + norm_back(lift_two_grad * vec_two[0], normed_two, inverse_two)
    middle_half = halved(middle_grad)
    out_bias_grad = jnp.sum(middle_grad, axis=0)
    middle_cols = lax.all_to_all(
        middle_half.reshape(slot_count, block_size, model_width), "seq", 2, 1, tiled=True
    ).reshape(all_rows, part_width)
    attended_back = halved(
        lax.dot_general(
            middle_cols, out_part, (((1,), (1,)), ((), ())), preferred_element_type=jnp.float32
        )
    )
    attended_grad = to_heads(
        lax.psum_scatter(
            jnp.transpose(attended_back.reshape(all_rows, groups, part_width), (1, 0, 2)),
            "seq",
            scatter_dimension=0,
            tiled=True,
        ).reshape(all_rows, part_width)
    )
    outward_part = outer(attended, middle_cols)
    delta_sum = jnp.sum(
        attended_grad.astype(jnp.float32) * attended_heads.astype(jnp.float32),
        axis=-1,
        keepdims=True,
    )
    weight_grad = jnp.einsum(
        "shqd,shkd->shqk", attended_grad, values, preferred_element_type=jnp.float32
    )
    score_grad = halved(weights_full * (weight_grad - delta_sum) * score_scale)
    query_grad = from_heads(
        jnp.einsum("shqk,shkd->shqd", score_grad, keys, preferred_element_type=jnp.float32)
    )
    key_grad = from_heads(
        jnp.einsum("shqk,shqd->shkd", score_grad, queries, preferred_element_type=jnp.float32)
    )
    value_grad = from_heads(
        jnp.einsum(
            "shqk,shqd->shkd", weights_half, attended_grad, preferred_element_type=jnp.float32
        )
    )
    packed_grad = halved(jnp.concatenate([query_grad, key_grad, value_grad], axis=1))
    lift_one_grad = scatter_rows(
        lax.dot_general(
            packed_grad, in_part, (((1,), (1,)), ((), ())), preferred_element_type=jnp.float32
        )
    )
    inward_part = outer(lifted_one, packed_grad)

    def place_part(part):
        return lax.dynamic_update_slice_in_dim(
            jnp.zeros((model_width,), jnp.float32), part, mine * part_width, 0
        )

    gain_one_grad = jnp.sum(lift_one_grad * normed_one, axis=0)
    shift_one_grad = jnp.sum(lift_one_grad, axis=0)
    tokens_grad = middle_grad + norm_back(lift_one_grad * vec_one[0], normed_one, inverse_one)
    input_gradient = tokens_grad.reshape(slot_count, block_size, model_width) * live_mask
    vector_grads = jnp.stack(
        [
            gain_one_grad,
            shift_one_grad,
            place_part(jnp.sum(query_grad, axis=0)),
            place_part(jnp.sum(value_grad, axis=0)),
            out_bias_grad,
            gain_two_grad,
            shift_two_grad,
            feed_bias_grad,
        ]
    ).reshape(8, devices, vec_width)
    bias_placed = lax.dynamic_update_slice_in_dim(
        jnp.zeros((replicas, groups, hidden_part), jnp.float32), bias_grad, mine, 1
    ).reshape(devices, hidden_part)
    small_grads = halved(
        jnp.concatenate(
            [jnp.transpose(vector_grads, (1, 0, 2)).reshape(devices, 8 * vec_width), bias_placed],
            axis=1,
        )
    ).reshape(replicas, groups, small_size)
    small_grads = jnp.pad(
        small_grads, ((0, 0), (0, pad_rows - groups), (0, model_width - small_size))
    )
    both_grads = jnp.concatenate([inward_part, outward_part], axis=1).reshape(
        replicas, block_rows, model_width
    )
    reduced = lax.psum_scatter(
        jnp.concatenate([both_grads, small_grads], axis=1).reshape(-1, model_width),
        "dp",
        scatter_dimension=0,
        tiled=True,
    )
    returned = lax.all_to_all(
        jnp.concatenate(
            [
                reduced[:block_rows].reshape(groups, in_rows, model_width),
                reduced[block_rows : block_rows + groups].reshape(groups, 1, model_width),
            ],
            axis=1,
        ),
        "seq",
        0,
        0,
        tiled=True,
    )
    both_sum = jnp.transpose(
        returned[:, :in_rows].reshape(groups, in_rows, -1, part_width), (1, 2, 0, 3)
    ).reshape(in_rows, -1).astype(jnp.float32)
    inward_sum = both_sum[:, : 3 * model_width]
    outward_sum = both_sum[:, 3 * model_width :]
    small_sum = jnp.sum(returned[:, in_rows, :small_size].astype(jnp.float32), axis=0)
    vector_sum = small_sum[: 8 * vec_width].reshape(8, vec_width)
    attend_vec_sum = vector_sum[:5]
    feed_vec_sum = vector_sum[5:]
    bias_sum = small_sum[8 * vec_width :]
    inward_new, inward_state = adamw_update(inward, inward_sum, inward_moments, weight_decay)
    outward_new, outward_state = adamw_update(outward, outward_sum, outward_moments, weight_decay)
    attend_new, attend_state = adamw_update(attend_vectors, attend_vec_sum, attend_moments, 0.0)
    expand_new, expand_state = adamw_update(expand, expand_sum, expand_moments, weight_decay)
    shrink_new, shrink_state = adamw_update(shrink, shrink_sum, shrink_moments, weight_decay)
    feed_new, feed_state = adamw_update(feed_vectors, feed_vec_sum, feed_moments, 0.0)
    bias_new, bias_state = adamw_update(expand_bias, bias_sum, bias_moments, 0.0)
    return (
        block_output,
        input_gradient,
        inward_sum,
        outward_sum,
        attend_vec_sum,
        expand_sum,
        shrink_sum,
        feed_vec_sum,
        bias_sum,
        inward_new,
        outward_new,
        attend_new,
        expand_new,
        shrink_new,
        feed_new,
        bias_new,
        inward_state,
        outward_state,
        attend_state,
        expand_state,
        shrink_state,
        feed_state,
        bias_state,
    )


def solution(mesh):
    placed = (
        P("dp", "seq", None),
        P("dp", "seq", None),
        P(),
        P(("dp", "seq"), None),
        P(("dp", "seq"), None),
        P(None, ("dp", "seq")),
        P(("dp", "seq"), None),
        P(("dp", "seq"), None),
        P(None, ("dp", "seq")),
        P(("dp", "seq")),
        P(None, ("dp", "seq"), None),
        P(None, ("dp", "seq"), None),
        P(None, None, ("dp", "seq")),
        P(None, ("dp", "seq"), None),
        P(None, ("dp", "seq"), None),
        P(None, None, ("dp", "seq")),
        P(None, ("dp", "seq")),
    )
    return jax.shard_map(
        body,
        mesh=mesh,
        in_specs=placed,
        out_specs=(
            P("dp", "seq", None),
            P("dp", "seq", None),
            P(("dp", "seq"), None),
            P(("dp", "seq"), None),
            P(None, ("dp", "seq")),
            P(("dp", "seq"), None),
            P(("dp", "seq"), None),
            P(None, ("dp", "seq")),
            P(("dp", "seq")),
            P(("dp", "seq"), None),
            P(("dp", "seq"), None),
            P(None, ("dp", "seq")),
            P(("dp", "seq"), None),
            P(("dp", "seq"), None),
            P(None, ("dp", "seq")),
            P(("dp", "seq")),
            P(None, ("dp", "seq"), None),
            P(None, ("dp", "seq"), None),
            P(None, None, ("dp", "seq")),
            P(None, ("dp", "seq"), None),
            P(None, ("dp", "seq"), None),
            P(None, None, ("dp", "seq")),
            P(None, ("dp", "seq")),
        ),
        check_vma=False,
    )
```
